32 devices in a mesh: dp: 8 (over y, x, core), hid: 4 (over z).
Axes of the slice: x: 2, y: 2, z: 4, core: 2. Of those that a mesh axis runs over, the one named last changes fastest.
Arguments:
- tokens: bfloat16 [512, 4096], P(('dp', 'hid')), may hold values from -6 to 6
- cotangent: bfloat16 [512, 7680], P('dp', 'hid'), may hold values from -8 to 8
- weights: bfloat16 [2, 7680, 4096], P(None, 'hid'), may hold values from -0.09375 to 0.09375
- basis: bfloat16 [4096, 256], P('dp'), may hold values from -0.09375 to 0.09375
- master: float32 [2, 7680, 4096], P(None, 'hid', 'dp'), may hold values from -0.09375 to 0.09375
- first_moment: float32 [7680, 2, 256], P(('hid', 'dp')), may hold values from -48 to 48
- second_moment: float32 [7680, 2, 256], P(('hid', 'dp')), may hold values from 25 to 2500
Outputs:
- master_new: float32 [2, 7680, 4096], P(None, 'hid', 'dp')
- first_new: float32 [7680, 2, 256], P(('hid', 'dp'))
- second_new: float32 [7680, 2, 256], P(('hid', 'dp'))
The draws below stay inside these ranges and needn't reach their ends.
All inputs are finite; a program needn't handle non-finite values.
Results may differ from the reference program's by a relative error of at most 0.0003.
Values may be sent and summed in bfloat16 or wider, within the bound.
No kernel may reach another device: no remote copies, remote signals or barrier semaphores. Data moves between devices by JAX's collectives and lax.ppermute only.
A program may use at most 128 MiB of HBM per device.

```python
import math
import jax
import jax.numpy as jnp
from jax import lax

D = 4096
FF = 7680
RANK = 256
GROUP_TOKENS = 64
TOKENS = 512
N_DP = 8


def with_spikes(array, rng, source, target, blocks, factor):
    owner, partner = [(jnp.arange(array.shape[dim]) // (array.shape[dim] // blocks)).reshape([-1 if axis == dim else 1 for axis in range(array.ndim)]) for dim in (source, target)]
    chosen = jax.random.permutation(rng, blocks)[partner]
    strong = (owner == chosen) | (owner == (partner + blocks // 2) % blocks)
    return jnp.where(strong, factor * array, array)


def steps_of(own_key, dims, cuts, least, largest):
    loudness = 1.0
    for dim, blocks in cuts:
        steps = jax.random.uniform(jax.random.fold_in(jax.random.fold_in(own_key, 6), dim), (blocks,), jnp.float32, least / len(cuts), largest / len(cuts))
        loudness = loudness * jnp.repeat(jnp.exp(steps), dims[dim] // blocks).reshape((-1,) + (1,) * (len(dims) - 1 - dim))
    return loudness


def gaussian(key, extent, spread, limit, split=(), kind=jnp.bfloat16):
    loudness = steps_of(key, extent, split, -0.22, 0.18) if split else 1.0
    result = jax.random.normal(key, extent, jnp.float32) * spread * loudness
    return jnp.minimum(jnp.maximum(result, -limit), limit).astype(kind)


def gaussian_with(key, dims, deviation, most, pieces, heavy, held_as=jnp.bfloat16):
    entries = deviation * jax.random.normal(key, dims, jnp.float32)
    if pieces:
        entries = entries * steps_of(key, dims, pieces, -0.22, 0.18)
    return jnp.clip(with_spikes(entries, jax.random.fold_in(key, 3), *heavy), -most, most).astype(held_as)


def setup_inputs(seed: int = 0) -> dict:
    key_list = jax.random.split(jax.random.key(seed), 8)
    return {
        "tokens": gaussian(key_list[0], (TOKENS, D), 1.0, 6.0, ((0, 32),)),
        "cotangent": gaussian_with(key_list[1], (TOKENS, FF), 1.0, 8.0, ((0, 8), (1, 4)), (0, 1, 8, 2.0)),
        "weights": gaussian(key_list[2], (2, FF, D), D ** -0.5, 0.09375, ((1, 4),)),
        "basis": gaussian(key_list[3], (D, RANK), D ** -0.5, 0.09375, ((0, 8),)),
        "master": gaussian(key_list[4], (2, FF, D), D ** -0.5, 0.09375, ((1, 4), (2, 8)), jnp.float32),
        "first_moment": gaussian(key_list[5], (FF, 2, RANK), 8.0, 48.0, ((0, 32),), jnp.float32),
        "second_moment": jnp.clip(jnp.exp(math.log(2500.0) - 4.6051702 * jax.random.uniform(key_list[6], (FF, 2, RANK), jnp.float32) ** steps_of(key_list[6], (FF, 2, RANK), ((0, 32),), -0.2, 0.2)), 25.0, 2500.0),
    }


beta_first = 0.9
beta_second = 0.95
step_size = 0.05
adam_epsilon = 1e-08

def silu_pieces(pre_gate):
    sigmoid_val = jax.nn.sigmoid(pre_gate)
    return (pre_gate * sigmoid_val, sigmoid_val * (1.0 + pre_gate * (1.0 - sigmoid_val)))

def reference(tokens, cotangent, weights, basis, master, first_moment, second_moment):
    highest = lax.Precision.HIGHEST
    token_groups = tokens.reshape(N_DP, GROUP_TOKENS, D)
    cot_groups = cotangent.reshape(N_DP, GROUP_TOKENS, FF)

    def add_group(running, inputs):
        group_tokens, group_cot = inputs
        pre_gate = jnp.dot(group_tokens, weights[0].T, preferred_element_type=jnp.float32)
        pre_up = jnp.dot(group_tokens, weights[1].T, preferred_element_type=jnp.float32)
        activated, silu_slope = silu_pieces(pre_gate)
        upstream = group_cot.astype(jnp.float32)
        grad_gate = upstream * pre_up * silu_slope
        grad_up = upstream * activated
        projected = jnp.dot(group_tokens, basis, preferred_element_type=jnp.float32)
        gate_term = jnp.dot(grad_gate.T, projected, precision=highest, preferred_element_type=jnp.float32)
        up_term = jnp.dot(grad_up.T, projected, precision=highest, preferred_element_type=jnp.float32)
        return (running + jnp.stack([gate_term, up_term], axis=1), None)
    gradient, unused = lax.scan(add_group, jnp.zeros((FF, 2, RANK), jnp.float32), (token_groups, cot_groups))
    first_new = beta_first * first_moment + (1.0 - beta_first) * gradient
    second_new = beta_second * second_moment + (1.0 - beta_second) * gradient * gradient
    direction = first_new / (jnp.sqrt(second_new) + adam_epsilon)
    basis_wide = basis.astype(jnp.float32)
    gate_lift = jnp.dot(direction[:, 0, :], basis_wide.T, precision=highest, preferred_element_type=jnp.float32)
    up_lift = jnp.dot(direction[:, 1, :], basis_wide.T, precision=highest, preferred_element_type=jnp.float32)
    master_new = master - step_size * jnp.stack([gate_lift, up_lift], axis=0)
    return (master_new, first_new, second_new)
```

```python
import functools

import jax
import jax.numpy as jnp
from jax import lax
from jax.experimental import pallas as pl
from jax.experimental.pallas import tpu as pltpu
from jax.sharding import PartitionSpec as P

beta_first = 0.9
beta_second = 0.95
step_size = 0.05
adam_epsilon = 1e-08
code_scale = 4096.0


VMEM = pl.BlockSpec(memory_space=pltpu.VMEM)
HBM = pl.BlockSpec(memory_space=pltpu.HBM)
MIB = 1 << 20


def silu_pieces(pre_gate):
    sigmoid_val = jax.nn.sigmoid(pre_gate)
    return (pre_gate * sigmoid_val, sigmoid_val * (1.0 + pre_gate * (1.0 - sigmoid_val)))


def split(x):
    high = x.astype(jnp.bfloat16)
    return high, (x - high.astype(jnp.float32)).astype(jnp.bfloat16)


def encode(x):
    a = jnp.abs(x) * code_scale
    a = a * a
    a = a * a
    a = a * a
    return jnp.where(x < 0, -a, a).astype(jnp.bfloat16)


def decode(y):
    y = y.astype(jnp.float32)
    a = jnp.abs(y)
    root = jnp.exp(0.125 * jnp.log(jnp.where(a == 0, 1.0, a))) * (1.0 / code_scale)
    root = jnp.where(a == 0, 0.0, root)
    return jnp.where(y < 0, -root, root)


def load_weights_kernel(share, places, w_hbm, out, sem):
    core = lax.rem(lax.axis_index("dp"), 2)
    plane = lax.div(lax.axis_index("dp"), 2)
    copies = []
    for j in range(places):
        row = pl.multiple_of((2 * jnp.bitwise_xor(plane, j) + core) * share, 16)
        copies.append(
            pltpu.make_async_copy(w_hbm.at[:, pl.ds(row, share)], out.at[j], sem.at[j])
        )
    for c in copies:
        c.start()
    for c in copies:
        c.wait()


def project_kernel(pieces, places, *refs):
    toks = refs[:pieces]
    bases = refs[pieces : pieces + places]
    out_tok, out_part, out_send = refs[pieces + places :]
    rows = toks[0].shape[0]
    core = lax.rem(lax.axis_index("dp"), 2)
    plane = lax.div(lax.axis_index("dp"), 2)
    for i, t in enumerate(toks):
        out_tok[i * rows : (i + 1) * rows] = t[...]
    depth = bases[0].shape[0]
    total = None
    for j in range(places):
        col = pl.multiple_of((2 * jnp.bitwise_xor(plane, j) + core) * depth, 128)
        term = jnp.dot(
            out_tok[:, pl.ds(col, depth)], bases[j][...], preferred_element_type=jnp.float32
        )
        total = term if total is None else total + term
    half = total.shape[0] // 2
    out_part[...] = total
    out_send[:half] = total[half:]
    out_send[half:] = total[:half]


def grads_kernel(j, n_hid, rows, tok, w, cot_own, cot_other, out):
    contract = (((1,), (1,)), ((), ()))
    plane = lax.div(lax.axis_index("dp"), 2)
    hid = lax.axis_index("hid")
    gate = lax.dot_general(tok[...], w[j, 0], contract, preferred_element_type=jnp.float32)
    up = lax.dot_general(tok[...], w[j, 1], contract, preferred_element_type=jnp.float32)
    place = jnp.bitwise_xor(plane, j)
    parts = []
    for cot in (cot_own, cot_other):
        for k in range(n_hid):
            start = pl.multiple_of(jnp.bitwise_xor(hid, k) * rows, rows)
            parts.append(cot[place, pl.ds(start, rows), :])
    upstream = jnp.concatenate(parts, axis=0).astype(jnp.float32)
    activated, slope = silu_pieces(gate)
    out[0] = upstream * up * slope
    out[1] = upstream * activated


def adam_kernel(places, *refs):
    grads = refs[:places]
    projs = refs[places : 2 * places]
    first, second, first_new, second_new, code = refs[2 * places :]
    over_tokens = (((0,), (0,)), ((), ()))
    p_high, p_low = split(jnp.concatenate([p[...] for p in projs], axis=0))
    for k in range(2):
        g_high, g_low = split(jnp.concatenate([g[k] for g in grads], axis=0))
        dot = functools.partial(
            lax.dot_general, dimension_numbers=over_tokens, preferred_element_type=jnp.float32
        )
        gradient = dot(g_high, p_high) + (dot(g_high, p_low) + dot(g_low, p_high))
        m = beta_first * first[k] + (1.0 - beta_first) * gradient
        v = beta_second * second[k] + (1.0 - beta_second) * gradient * gradient
        first_new[k] = m
        second_new[k] = v
        code[k] = encode(m / (jnp.sqrt(v) + adam_epsilon))


def lift_kernel(share, places, *refs):
    codes = refs[: 2 * places]
    basis, master, out, m_buf, o_buf, in_sem, out_sem = refs[2 * places :]
    core = lax.rem(lax.axis_index("dp"), 2)
    plane = lax.div(lax.axis_index("dp"), 2)
    contract = (((1,), (1,)), ((), ()))
    ins, outs = [], []
    for i in range(2 * places):
        j, other = i // 2, i % 2
        who = 2 * jnp.bitwise_xor(plane, j) + jnp.bitwise_xor(core, other)
        row = pl.ds(pl.multiple_of(who * share, 16), share)
        ins.append(pltpu.make_async_copy(master.at[:, row], m_buf.at[i], in_sem.at[i]))
        outs.append(pltpu.make_async_copy(o_buf.at[i], out.at[:, row], out_sem.at[i]))
    for c in ins:
        c.start()
    for i in range(2 * places):
        ins[i].wait()
        for k in range(2):
            high, low = split(decode(codes[i][k]))
            lifted = lax.dot_general(
                high, basis[...], contract, preferred_element_type=jnp.float32
            ) + lax.dot_general(low, basis[...], contract, preferred_element_type=jnp.float32)
            o_buf[i, k] = m_buf[i, k] - step_size * lifted
        outs[i].start()
    for c in outs:
        c.wait()


def fast_device(n_dp, n_hid, tokens, cotangent, weights, basis, master, first_moment, second_moment):
    places = n_dp // 2
    rows, width = tokens.shape
    group = rows * n_hid
    ff = weights.shape[1]
    share = ff // n_dp
    depth, rank = basis.shape
    f32, bf16 = jnp.float32, jnp.bfloat16

    def swap_hid(x, k):
        return lax.ppermute(x, "hid", [(i, i ^ k) for i in range(n_hid)])

    def swap_plane(x, j):
        return lax.ppermute(x, "dp", [(i, i ^ (2 * j)) for i in range(n_dp)])

    def swap_core(x):
        return lax.ppermute(x, "dp", [(i, i ^ 1) for i in range(n_dp)])

    core = lax.rem(lax.axis_index("dp"), 2)

    own = [tokens] + [swap_hid(tokens, k) for k in range(n_hid - 1, 0, -1)][::-1]
    bases = [basis] + [swap_plane(basis, j) for j in range(1, places)]
    other = [swap_core(t) for t in own]

    cot = cotangent.reshape(group, places, 2, share).transpose(2, 1, 0, 3)
    cot_own = lax.dynamic_index_in_dim(cot, core, 0, keepdims=False)
    cot_other = swap_core(lax.dynamic_index_in_dim(cot, 1 - core, 0, keepdims=False))

    held = pl.pallas_call(
        functools.partial(load_weights_kernel, share, places),
        in_specs=[HBM],
        out_specs=VMEM,
        out_shape=pltpu.VMEM((places, 2, share, width), bf16),
        scratch_shapes=[pltpu.SemaphoreType.DMA((places,))],
        compiler_params=pltpu.CompilerParams(vmem_limit_bytes=MIB),
        cost_estimate=pl.CostEstimate(
            flops=0, bytes_accessed=2 * places * 2 * share * width * 2, transcendentals=0
        ),
        name="load_weights",
    )(pltpu.with_memory_space_constraint(weights, pltpu.HBM))

    part_shape = jax.ShapeDtypeStruct((2 * group, rank), f32)
    toks, part, part_send = pl.pallas_call(
        functools.partial(project_kernel, 2 * n_hid, places),
        in_specs=[VMEM] * (2 * n_hid + places),
        out_specs=[VMEM] * 3,
        out_shape=[
            jax.ShapeDtypeStruct((2 * group, width), bf16),
            part_shape,
            part_shape,
        ],
        compiler_params=pltpu.CompilerParams(vmem_limit_bytes=16 * MIB),
        cost_estimate=pl.CostEstimate(
            flops=2 * 2 * group * places * depth * rank,
            bytes_accessed=4 * group * width * 2,
            transcendentals=0,
        ),
        name="project",
    )(*own, *other, *bases)
    projected = part + swap_core(part_send)

    grads, projs = [], []
    for j in range(places - 1, -1, -1):
        g = pl.pallas_call(
            functools.partial(grads_kernel, j, n_hid, rows),
            in_specs=[VMEM] * 4,
            out_specs=VMEM,
            out_shape=jax.ShapeDtypeStruct((2, 2 * group, share), f32),
            compiler_params=pltpu.CompilerParams(vmem_limit_bytes=16 * MIB),
            cost_estimate=pl.CostEstimate(
                flops=2 * 2 * group * 2 * share * width,
                bytes_accessed=2 * share * width * 2,
                transcendentals=2 * group * share,
            ),
            name=f"grads{j}",
        )(toks, held, cot_own, cot_other)
        grads.append(swap_plane(g, j) if j else g)
        projs.append(swap_plane(projected, j) if j else projected)

    first_t = first_moment.transpose(1, 0, 2)
    second_t = second_moment.transpose(1, 0, 2)
    half = jax.ShapeDtypeStruct((2, share, rank), f32)
    first_new, second_new, code = pl.pallas_call(
        functools.partial(adam_kernel, places),
        in_specs=[VMEM] * (2 * places + 2),
        out_specs=[VMEM] * 3,
        out_shape=[half, half, jax.ShapeDtypeStruct((2, share, rank), bf16)],
        compiler_params=pltpu.CompilerParams(vmem_limit_bytes=24 * MIB),
        cost_estimate=pl.CostEstimate(
            flops=6 * 2 * 2 * share * rank * places * 2 * group,
            bytes_accessed=2 * share * rank * 20,
            transcendentals=2 * share * rank,
        ),
        name="adam",
    )(*grads, *projs, first_t, second_t)

    codes = []
    for j in range(places):
        c = swap_plane(code, j) if j else code
        codes += [c, swap_core(c)]
    block = (2 * places, 2, share, depth)
    master_new = pl.pallas_call(
        functools.partial(lift_kernel, share, places),
        in_specs=[VMEM] * (2 * places + 1) + [HBM],
        out_specs=HBM,
        out_shape=jax.ShapeDtypeStruct(master.shape, f32),
        scratch_shapes=[
            pltpu.VMEM(block, f32),
            pltpu.VMEM(block, f32),
            pltpu.SemaphoreType.DMA((2 * places,)),
            pltpu.SemaphoreType.DMA((2 * places,)),
        ],
        compiler_params=pltpu.CompilerParams(vmem_limit_bytes=40 * MIB),
        cost_estimate=pl.CostEstimate(
            flops=2 * 2 * 2 * ff * rank * depth,
            bytes_accessed=2 * 2 * ff * depth * 4,
            transcendentals=4 * ff * rank,
        ),
        name="lift",
    )(*codes, basis, master)
    return master_new, first_new.transpose(1, 0, 2), second_new.transpose(1, 0, 2)


def plain_device(tokens, cotangent, weights, basis, master, first_moment, second_moment):
    highest = lax.Precision.HIGHEST
    group_tokens = lax.all_gather(tokens, "hid", axis=0, tiled=True)
    projected = jnp.dot(
        group_tokens,
        lax.all_gather(basis, "dp", axis=0, tiled=True),
        preferred_element_type=jnp.float32,
    )
    contract_cols = (((1,), (1,)), ((), ()))
    pre_gate = lax.dot_general(
        group_tokens, weights[0], contract_cols, preferred_element_type=jnp.float32
    )
    pre_up = lax.dot_general(
        group_tokens, weights[1], contract_cols, preferred_element_type=jnp.float32
    )
    activated, silu_slope = silu_pieces(pre_gate)
    upstream = cotangent.astype(jnp.float32)
    grad_gate = upstream * pre_up * silu_slope
    grad_up = upstream * activated
    over_tokens = (((0,), (0,)), ((), ()))
    gate_term = lax.dot_general(
        grad_gate, projected, over_tokens, precision=highest, preferred_element_type=jnp.float32
    )
    up_term = lax.dot_general(
        grad_up, projected, over_tokens, precision=highest, preferred_element_type=jnp.float32
    )
    gradient = lax.psum_scatter(
        jnp.stack([gate_term, up_term], axis=1), "dp", scatter_dimension=0, tiled=True
    )
    first_new = beta_first * first_moment + (1.0 - beta_first) * gradient
    second_new = beta_second * second_moment + (1.0 - beta_second) * gradient * gradient
    direction_share = first_new / (jnp.sqrt(second_new) + adam_epsilon)
    direction = lax.all_gather(direction_share, "dp", axis=0, tiled=True)
    lifted = jnp.einsum("fwr,dr->wfd", direction, basis.astype(jnp.float32), precision=highest)
    master_new = master - step_size * lifted
    return (master_new, first_new, second_new)


def power_of_two(n):
    return n & (n - 1) == 0


def solution(mesh):
    n_dp, n_hid = mesh.shape["dp"], mesh.shape["hid"]

    def on_device(tokens, cotangent, weights, *rest):
        share = weights.shape[1] // n_dp
        aligned = share % 16 == 0 and tokens.shape[0] % 16 == 0 and rest[0].shape[0] % 128 == 0
        few = power_of_two(n_dp) and power_of_two(n_hid) and 2 < n_dp <= 16 and n_hid <= 8
        if aligned and few:
            return fast_device(n_dp, n_hid, tokens, cotangent, weights, *rest)
        return plain_device(tokens, cotangent, weights, *rest)

    in_specs = (
        P(("dp", "hid"), None),
        P("dp", "hid"),
        P(None, "hid", None),
        P("dp", None),
        P(None, "hid", "dp"),
        P(("hid", "dp"), None, None),
        P(("hid", "dp"), None, None),
    )
    out_specs = (P(None, "hid", "dp"), P(("hid", "dp"), None, None), P(("hid", "dp"), None, None))
    return jax.shard_map(
        on_device, mesh=mesh, in_specs=in_specs, out_specs=out_specs, check_vma=False
    )
```

```python
import functools

import jax
import jax.numpy as jnp
from jax import lax
from jax.experimental import pallas as pl
from jax.experimental.pallas import tpu as pltpu
from jax.sharding import PartitionSpec as P


beta_first = 0.9
beta_second = 0.95
step_size = 0.05
adam_epsilon = 1e-08
code_scale = 4096.0
code_scale_squarings = 3
code_top = 240.0
code_squarings = 4
tiny = 1e-30


VMEM = pl.BlockSpec(memory_space=pltpu.VMEM)
HBM = pl.BlockSpec(memory_space=pltpu.HBM)
MIB = 1 << 20


def silu_pieces(pre_gate):
    sigmoid_val = jax.nn.sigmoid(pre_gate)
    return (pre_gate * sigmoid_val, sigmoid_val * (1.0 + pre_gate * (1.0 - sigmoid_val)))


def split(x):
    high = x.astype(jnp.bfloat16)
    return high, (x - high.astype(jnp.float32)).astype(jnp.bfloat16)


def encode(x, scale, squarings):
    a = jnp.abs(x) * scale
    for _ in range(squarings):
        a = a * a
    return jnp.where(x < 0, -a, a).astype(jnp.bfloat16)


def decode(y, inverse_scale, squarings):
    a = jnp.abs(y)
    root = jnp.exp(jnp.log(jnp.where(a == 0, 1.0, a)) * 0.5**squarings) * inverse_scale
    root = jnp.where(a == 0, 0.0, root)
    return jnp.where(y < 0, -root, root)


def scale_for(*terms):
    most = functools.reduce(jnp.maximum, [jnp.max(jnp.abs(t)) for t in terms])
    return (code_top / jnp.maximum(jnp.full((1, 1), most), tiny)).astype(jnp.bfloat16)


def load_weights_kernel(share, places, w_hbm, out, sem):
    core = lax.rem(lax.axis_index("dp"), 2)
    plane = lax.div(lax.axis_index("dp"), 2)
    copies = []
    for j in range(places):
        row = pl.multiple_of((2 * jnp.bitwise_xor(plane, j) + core) * share, 16)
        copies.append(
            pltpu.make_async_copy(w_hbm.at[:, pl.ds(row, share)], out.at[j], sem.at[j])
        )
    for c in copies:
        c.start()
    for c in copies:
        c.wait()


def cotangents_kernel(share, places, cot, own, send):
    core = lax.rem(lax.axis_index("dp"), 2)
    for c in range(2):

        @pl.when(core == c)
        def _():
            for p in range(places):
                here, there = 2 * p + c, 2 * p + 1 - c
                own[p] = cot[:, here * share : (here + 1) * share]
                send[p] = cot[:, there * share : (there + 1) * share]


def project_kernel(places, tok, *refs):
    bases = refs[:places]
    out_part, out_send = refs[places:]
    core = lax.rem(lax.axis_index("dp"), 2)
    plane = lax.div(lax.axis_index("dp"), 2)
    depth = bases[0].shape[0]
    total = None
    for j in range(places):
        col = pl.multiple_of((2 * jnp.bitwise_xor(plane, j) + core) * depth, 128)
        term = jnp.dot(tok[:, pl.ds(col, depth)], bases[j][...], preferred_element_type=jnp.float32)
        total = term if total is None else total + term
    half = total.shape[0] // 2
    out_part[...] = total
    out_send[:half] = total[half:]
    out_send[half:] = total[:half]


def grads_kernel(j, n_hid, rows, with_tokens, with_projected, extra_projected, *refs):
    refs = list(refs)
    pieces = 2 * n_hid if with_tokens else 1
    toks, (w, cot_own, cot_other) = refs[:pieces], refs[pieces : pieces + 3]
    refs = refs[pieces + 3 :]
    part, part_other = (refs.pop(0), refs.pop(0)) if with_projected else (None, None)
    out = refs[0]
    tok = toks[0]
    if with_tokens:
        tok = refs[1]
        for i, t in enumerate(toks):
            tok[i * rows : (i + 1) * rows] = t[...]
    contract = (((1,), (1,)), ((), ()))
    plane = lax.div(lax.axis_index("dp"), 2)
    hid = lax.axis_index("hid")
    gate = lax.dot_general(tok[...], w[j, 0], contract, preferred_element_type=jnp.float32)
    up = lax.dot_general(tok[...], w[j, 1], contract, preferred_element_type=jnp.float32)
    place = jnp.bitwise_xor(plane, j)
    parts = []
    for cot in (cot_own, cot_other):
        for k in range(n_hid):
            start = pl.multiple_of(jnp.bitwise_xor(hid, k) * rows, rows)
            parts.append(cot[place, pl.ds(start, rows), :])
    upstream = jnp.concatenate(parts, axis=0).astype(jnp.float32)
    activated, slope = silu_pieces(gate)
    terms = (upstream * up * slope, upstream * activated)
    n_tok, share = gate.shape
    if j == 0:
        out[0], out[1] = terms
        return
    scale = scale_for(*terms)
    wide = scale.astype(jnp.float32)
    for k in range(2):
        here = slice(k * n_tok, (k + 1) * n_tok)
        out[here, :share] = encode(terms[k], wide, code_squarings)
        out[here, share:] = jnp.broadcast_to(scale, (n_tok, out.shape[1] - share))
    if with_projected:
        projected = part[...] + part_other[...]
        scale = scale_for(projected)
        coded = encode(projected, scale.astype(jnp.float32), code_squarings)
        for ref, top in [(out, 2 * n_tok)] + ([(refs[1], 0)] if extra_projected else []):
            ref[top : top + n_tok] = coded
            ref[top + n_tok :] = jnp.broadcast_to(scale, (ref.shape[0] - top - n_tok, ref.shape[1]))


def adam_kernel(places, share, own_grads, part, part_other, *refs):
    messages = refs[: places - 1]
    last_projected, first, second, first_new, second_new, code = refs[places - 1 :]
    n_tok = part.shape[0]
    dot = functools.partial(
        lax.dot_general,
        dimension_numbers=(((0,), (0,)), ((), ())),
        preferred_element_type=jnp.float32,
    )
    projs = [part[...] + part_other[...]]
    for i, m in enumerate(messages):
        ref, top = (m, 2 * n_tok) if i < places - 2 else (last_projected, 0)
        values = ref[top : top + n_tok].astype(jnp.float32)
        scale = ref[top + n_tok : top + n_tok + 1, :].astype(jnp.float32)
        projs.append(decode(values, 1.0 / scale, code_squarings))
    p_high, p_low = split(jnp.concatenate(projs, axis=0))
    for k in range(2):
        parts = [own_grads[k]]
        for m in messages:
            values = m[k * n_tok : (k + 1) * n_tok].astype(jnp.float32)
            scale = values[:, share : share + 1]
            parts.append(decode(values, 1.0 / scale, code_squarings)[:, :share])
        g_high, g_low = split(jnp.concatenate(parts, axis=0))
        gradient = dot(g_high, p_high) + (dot(g_high, p_low) + dot(g_low, p_high))
        m = beta_first * first[k] + (1.0 - beta_first) * gradient
        v = beta_second * second[k] + (1.0 - beta_second) * gradient * gradient
        first_new[k] = m
        second_new[k] = v
        code[k] = encode(m / (jnp.sqrt(v) + adam_epsilon), code_scale, code_scale_squarings)


def moments_kernel(first, second, first_out, second_out):
    for k in range(2):
        first_out[:, k] = first[k]
        second_out[:, k] = second[k]


def load_master_kernel(pieces, hbm, out, sem):
    rows = out.shape[1] // pieces
    copies = []
    for i in range(pieces):
        at = (slice(None), pl.ds(i * rows, rows))
        copies.append(pltpu.make_async_copy(hbm.at[at], out.at[at], sem.at[i]))
    for c in copies:
        c.start()
    for c in copies:
        c.wait()


def lift_kernel(share, j, other, *refs):
    codes, basis, master = refs[:3]
    out, o_buf, sem = refs[-3:]
    core = lax.rem(lax.axis_index("dp"), 2)
    plane = lax.div(lax.axis_index("dp"), 2)
    who = 2 * jnp.bitwise_xor(plane, j) + jnp.bitwise_xor(core, other)
    row = pl.ds(pl.multiple_of(who * share, 16), share)
    copies = []
    for k in range(2):
        values = codes[k].astype(jnp.float32)
        terms = split(decode(values, step_size / code_scale, code_scale_squarings))
        lifted = jnp.dot(
            jnp.concatenate(terms, axis=1), basis[...], preferred_element_type=jnp.float32
        )
        o_buf[k] = master[k, row, :] - lifted
        c = pltpu.make_async_copy(o_buf.at[k], out.at[k, row], sem.at[k])
        c.start()
        copies.append(c)
    for c in copies:
        c.wait()


def fast_device(n_dp, n_hid, tokens, cotangent, weights, basis, master, first_moment, second_moment):
    places = n_dp // 2
    rows, width = tokens.shape
    group = rows * n_hid
    ff = weights.shape[1]
    share = ff // n_dp
    depth, rank = basis.shape
    f32, bf16 = jnp.float32, jnp.bfloat16

    def swap(x, axis, flip):
        n = n_hid if axis == "hid" else n_dp
        return lax.ppermute(x, axis, [(i, i ^ flip) for i in range(n)])

    def swap_hid(x, k):
        return swap(x, "hid", k)

    def swap_plane(x, j):
        return swap(x, "dp", 2 * j) if j else x

    def swap_core(x):
        return swap(x, "dp", 1)

    core = lax.rem(lax.axis_index("dp"), 2)

    own = [tokens] + [swap_hid(tokens, k) for k in range(n_hid - 1, 0, -1)][::-1]
    bases = [basis] + [swap_plane(basis, j) for j in range(1, places)]

    cot_shape = jax.ShapeDtypeStruct((places, group, share), bf16)
    cot_own, cot_send = pl.pallas_call(
        functools.partial(cotangents_kernel, share, places),
        in_specs=[VMEM],
        out_specs=[VMEM] * 2,
        out_shape=[cot_shape] * 2,
        compiler_params=pltpu.CompilerParams(vmem_limit_bytes=4 * MIB),
        name="cotangents",
    )(cotangent)
    cot_other = swap_core(cot_send)

    held = pl.pallas_call(
        functools.partial(load_weights_kernel, share, places),
        in_specs=[HBM],
        out_specs=VMEM,
        out_shape=pltpu.VMEM((places, 2, share, width), bf16),
        scratch_shapes=[pltpu.SemaphoreType.DMA((places,))],
        compiler_params=pltpu.CompilerParams(vmem_limit_bytes=MIB),
        cost_estimate=pl.CostEstimate(
            flops=0, bytes_accessed=2 * places * 2 * share * width * 2, transcendentals=0
        ),
        name="load_weights",
    )(pltpu.with_memory_space_constraint(weights, pltpu.HBM))

    other = [swap_core(t) for t in own]
    messages, part, part_other = {}, None, None
    n_tok, spare = 2 * group, 16
    for j in [places - 1, 0] + list(range(places - 2, 0, -1)):
        first, extra = j == places - 1, j == places - 2
        with_projected = bool(j) and not first
        ins = (own + other if first else [toks]) + [held, cot_own, cot_other]
        ins += [part, part_other] if with_projected else []
        if not j:
            shapes = [jax.ShapeDtypeStruct((2, n_tok, share), f32)]
        else:
            depth_of = 2 * n_tok + (n_tok + spare if with_projected else 0)
            shapes = [jax.ShapeDtypeStruct((depth_of, rank), bf16)]
        if first:
            shapes.append(jax.ShapeDtypeStruct((n_tok, width), bf16))
        if extra:
            shapes.append(jax.ShapeDtypeStruct((n_tok + spare, rank), bf16))
        outs = pl.pallas_call(
            functools.partial(grads_kernel, j, n_hid, rows, first, with_projected, extra),
            in_specs=[VMEM] * len(ins),
            out_specs=[VMEM] * len(shapes),
            out_shape=shapes,
            compiler_params=pltpu.CompilerParams(vmem_limit_bytes=16 * MIB),
            cost_estimate=pl.CostEstimate(
                flops=2 * n_tok * 2 * share * width,
                bytes_accessed=2 * share * width * 2,
                transcendentals=n_tok * share,
            ),
        )(*ins)
        messages[j] = swap_plane(outs[0], j)
        if first:
            toks = outs[1]
            part_shape = jax.ShapeDtypeStruct((n_tok, rank), f32)
            part, part_send = pl.pallas_call(
                functools.partial(project_kernel, places),
                in_specs=[VMEM] * (1 + places),
                out_specs=[VMEM] * 2,
                out_shape=[part_shape] * 2,
                compiler_params=pltpu.CompilerParams(vmem_limit_bytes=16 * MIB),
                cost_estimate=pl.CostEstimate(
                    flops=2 * n_tok * places * depth * rank,
                    bytes_accessed=n_tok * width * 2,
                    transcendentals=0,
                ),
                name="project",
            )(toks, *bases)
            part_other = swap_core(part_send)
        if extra:
            last_projected = swap_plane(outs[1], places - 1)

    half = jax.ShapeDtypeStruct((2, share, rank), f32)
    first_new, second_new, code = pl.pallas_call(
        functools.partial(adam_kernel, places, share),
        in_specs=[VMEM] * (places + 5),
        out_specs=[VMEM] * 3,
        out_shape=[half, half, jax.ShapeDtypeStruct((2, share, rank), bf16)],
        compiler_params=pltpu.CompilerParams(vmem_limit_bytes=24 * MIB),
        cost_estimate=pl.CostEstimate(
            flops=6 * 2 * 2 * share * rank * places * 2 * group,
            bytes_accessed=2 * share * rank * 20,
            transcendentals=2 * share * rank,
        ),
        name="adam",
    )(
        messages[0],
        part,
        part_other,
        *[messages[j] for j in range(1, places)],
        last_projected,
        first_moment.transpose(1, 0, 2),
        second_moment.transpose(1, 0, 2),
    )

    codes = [swap_plane(code, j) for j in range(places - 1)]
    relay = jnp.where(core == 0, codes[1], codes[2])
    flips = [4 if i % 2 == 0 else 2 for i in range(n_dp)]
    codes.append(lax.ppermute(relay, "dp", [(i, i ^ flips[i]) for i in range(n_dp)]))
    moment_shape = jax.ShapeDtypeStruct((share, 2, rank), f32)
    first_new, second_new = pl.pallas_call(
        moments_kernel,
        in_specs=[VMEM] * 2,
        out_specs=[VMEM] * 2,
        out_shape=[moment_shape] * 2,
        compiler_params=pltpu.CompilerParams(vmem_limit_bytes=8 * MIB),
        name="moments",
    )(first_new, second_new)
    master = pl.pallas_call(
        functools.partial(load_master_kernel, places),
        in_specs=[HBM],
        out_specs=VMEM,
        out_shape=pltpu.VMEM(master.shape, f32),
        scratch_shapes=[pltpu.SemaphoreType.DMA((places,))],
        compiler_params=pltpu.CompilerParams(vmem_limit_bytes=MIB),
        cost_estimate=pl.CostEstimate(
            flops=0, bytes_accessed=2 * 2 * ff * depth * 4, transcendentals=0
        ),
        name="load_master",
    )(pltpu.with_memory_space_constraint(master, pltpu.HBM))
    basis_twice = jnp.concatenate([basis.T, basis.T], axis=0)
    master_new = None
    for j in range(places):
        for o, c in enumerate((codes[j], swap_core(codes[j]))):
            kept = () if master_new is None else (master_new,)
            master_new = pl.pallas_call(
                functools.partial(lift_kernel, share, j, o),
                in_specs=[VMEM] * 3 + [HBM] * len(kept),
                out_specs=HBM,
                out_shape=jax.ShapeDtypeStruct(master.shape, f32),
                scratch_shapes=[
                    pltpu.VMEM((2, share, depth), f32),
                    pltpu.SemaphoreType.DMA((2,)),
                ],
                input_output_aliases={3: 0} if kept else {},
                compiler_params=pltpu.CompilerParams(vmem_limit_bytes=16 * MIB),
                cost_estimate=pl.CostEstimate(
                    flops=2 * 2 * 2 * share * rank * depth,
                    bytes_accessed=2 * 2 * share * depth * 4,
                    transcendentals=4 * share * rank,
                ),
            )(c, basis_twice, master, *kept)
    return master_new, first_new, second_new


def plain_device(tokens, cotangent, weights, basis, master, first_moment, second_moment):
    highest = lax.Precision.HIGHEST
    group_tokens = lax.all_gather(tokens, "hid", axis=0, tiled=True)
    projected = jnp.dot(
        group_tokens,
        lax.all_gather(basis, "dp", axis=0, tiled=True),
        preferred_element_type=jnp.float32,
    )
    contract_cols = (((1,), (1,)), ((), ()))
    pre_gate = lax.dot_general(
        group_tokens, weights[0], contract_cols, preferred_element_type=jnp.float32
    )
    pre_up = lax.dot_general(
        group_tokens, weights[1], contract_cols, preferred_element_type=jnp.float32
    )
    activated, silu_slope = silu_pieces(pre_gate)
    upstream = cotangent.astype(jnp.float32)
    grad_gate = upstream * pre_up * silu_slope
    grad_up = upstream * activated
    over_tokens = (((0,), (0,)), ((), ()))
    gate_term = lax.dot_general(
        grad_gate, projected, over_tokens, precision=highest, preferred_element_type=jnp.float32
    )
    up_term = lax.dot_general(
        grad_up, projected, over_tokens, precision=highest, preferred_element_type=jnp.float32
    )
    gradient = lax.psum_scatter(
        jnp.stack([gate_term, up_term], axis=1), "dp", scatter_dimension=0, tiled=True
    )
    first_new = beta_first * first_moment + (1.0 - beta_first) * gradient
    second_new = beta_second * second_moment + (1.0 - beta_second) * gradient * gradient
    direction_share = first_new / (jnp.sqrt(second_new) + adam_epsilon)
    direction = lax.all_gather(direction_share, "dp", axis=0, tiled=True)
    lifted = jnp.einsum("fwr,dr->wfd", direction, basis.astype(jnp.float32), precision=highest)
    master_new = master - step_size * lifted
    return (master_new, first_new, second_new)


def power_of_two(n):
    return n & (n - 1) == 0


def solution(mesh):
    n_dp, n_hid = mesh.shape["dp"], mesh.shape["hid"]

    def on_device(tokens, cotangent, weights, *rest):
        share = weights.shape[1] // n_dp
        aligned = share % 16 == 0 and tokens.shape[0] % 16 == 0 and rest[0].shape[0] % 128 == 0
        aligned = aligned and rest[0].shape[1] == (share // 128 + 1) * 128
        few = n_dp == 8 and power_of_two(n_hid) and n_hid <= 8
        if aligned and few:
            return fast_device(n_dp, n_hid, tokens, cotangent, weights, *rest)
        return plain_device(tokens, cotangent, weights, *rest)

    in_specs = (
        P(("dp", "hid"), None),
        P("dp", "hid"),
        P(None, "hid", None),
        P("dp", None),
        P(None, "hid", "dp"),
        P(("hid", "dp"), None, None),
        P(("hid", "dp"), None, None),
    )
    out_specs = (P(None, "hid", "dp"), P(("hid", "dp"), None, None), P(("hid", "dp"), None, None))
    return jax.shard_map(
        on_device, mesh=mesh, in_specs=in_specs, out_specs=out_specs, check_vma=False
    )
```

```python
import functools

import jax
import jax.numpy as jnp
from jax import lax
from jax.experimental import pallas as pl
from jax.experimental.pallas import tpu as pltpu
from jax.sharding import PartitionSpec as P


beta_first = 0.9
beta_second = 0.95
step_size = 0.05
adam_epsilon = 1e-08
code_scale = 4096.0
code_scale_squarings = 3
code_top = 240.0
code_squarings = 4
tiny = 1e-30


VMEM = pl.BlockSpec(memory_space=pltpu.VMEM)
HBM = pl.BlockSpec(memory_space=pltpu.HBM)
SMALL = pl.CostEstimate(flops=1000, bytes_accessed=1000, transcendentals=0)
MIB = 1 << 20


def silu_pieces(pre_gate):
    sigmoid_val = jax.nn.sigmoid(pre_gate)
    return (pre_gate * sigmoid_val, sigmoid_val * (1.0 + pre_gate * (1.0 - sigmoid_val)))


def split(x):
    high = x.astype(jnp.bfloat16)
    return high, (x - high.astype(jnp.float32)).astype(jnp.bfloat16)


def encode(x, scale, squarings):
    a = jnp.abs(x) * scale
    for _ in range(squarings):
        a = a * a
    return jnp.where(x < 0, -a, a).astype(jnp.bfloat16)


def decode(y, inverse_scale, squarings):
    a = jnp.abs(y)
    root = jnp.exp(jnp.log(a) * 0.5**squarings) * inverse_scale
    return jnp.where(y < 0, -root, root)


def scale_for(*terms):
    most = functools.reduce(jnp.maximum, [jnp.max(jnp.abs(t)) for t in terms])
    return (code_top / jnp.maximum(jnp.full((1, 1), most), tiny)).astype(jnp.bfloat16)


def load_weights_kernel(share, places, w_hbm, out, sem):
    core = lax.rem(lax.axis_index("dp"), 2)
    plane = lax.div(lax.axis_index("dp"), 2)
    copies = []
    for j in range(places):
        row = pl.multiple_of((2 * jnp.bitwise_xor(plane, j) + core) * share, 16)
        copies.append(
            pltpu.make_async_copy(w_hbm.at[:, pl.ds(row, share)], out.at[j], sem.at[j])
        )
    for c in copies:
        c.start()
    for c in copies:
        c.wait()


def cotangents_kernel(share, places, cot, own, send):
    core = lax.rem(lax.axis_index("dp"), 2)
    for c in range(2):

        @pl.when(core == c)
        def _():
            for p in range(places):
                here, there = 2 * p + c, 2 * p + 1 - c
                own[p] = cot[:, here * share : (here + 1) * share]
                send[p] = cot[:, there * share : (there + 1) * share]


def project_kernel(places, tok, *refs):
    bases = refs[:places]
    out_part, out_send = refs[places:]
    core = lax.rem(lax.axis_index("dp"), 2)
    plane = lax.div(lax.axis_index("dp"), 2)
    depth = bases[0].shape[0]
    total = None
    for j in range(places):
        col = pl.multiple_of((2 * jnp.bitwise_xor(plane, j) + core) * depth, 128)
        term = jnp.dot(tok[:, pl.ds(col, depth)], bases[j][...], preferred_element_type=jnp.float32)
        total = term if total is None else total + term
    half = total.shape[0] // 2
    out_part[...] = total
    out_send[:half] = total[half:]
    out_send[half:] = total[:half]


def grads_kernel(j, n_hid, rows, with_tokens, *refs):
    pieces = 2 * n_hid if with_tokens else 1
    toks, (w, cot_own, cot_other) = refs[:pieces], refs[pieces : pieces + 3]
    out = refs[pieces + 3]
    tok = toks[0]
    if with_tokens:
        tok = refs[-1]
        for i, t in enumerate(toks):
            tok[i * rows : (i + 1) * rows] = t[...]
    contract = (((1,), (1,)), ((), ()))
    plane = lax.div(lax.axis_index("dp"), 2)
    hid = lax.axis_index("hid")
    gate = lax.dot_general(tok[...], w[j, 0], contract, preferred_element_type=jnp.float32)
    up = lax.dot_general(tok[...], w[j, 1], contract, preferred_element_type=jnp.float32)
    place = jnp.bitwise_xor(plane, j)
    parts = []
    for cot in (cot_own, cot_other):
        for k in range(n_hid):
            start = pl.multiple_of(jnp.bitwise_xor(hid, k) * rows, rows)
            parts.append(cot[place, pl.ds(start, rows), :])
    upstream = jnp.concatenate(parts, axis=0).astype(jnp.float32)
    activated, slope = silu_pieces(gate)
    terms = (upstream * up * slope, upstream * activated)
    n_tok, share = gate.shape
    if j == 0:
        out[0], out[1] = terms
        return
    scale = scale_for(*terms)
    wide = scale.astype(jnp.float32)
    for k in range(2):
        here = slice(k * n_tok, (k + 1) * n_tok)
        out[here, :share] = encode(terms[k], wide, code_squarings)
        out[here, share:] = jnp.broadcast_to(scale, (n_tok, out.shape[1] - share))


def code_projected_kernel(part, part_other, basis, out, basis_twice):
    n_tok = part.shape[0]
    projected = part[...] + part_other[...]
    scale = scale_for(projected)
    out[:n_tok] = encode(projected, scale.astype(jnp.float32), code_squarings)
    out[n_tok:] = jnp.broadcast_to(scale, (out.shape[0] - n_tok, out.shape[1]))
    turned = basis[...].T
    rank = turned.shape[0]
    basis_twice[:rank] = turned
    basis_twice[rank:] = turned


def adam_kernel(places, share, own_grads, part, part_other, *refs):
    messages, coded = refs[: places - 1], refs[places - 1 : 2 * places - 2]
    first, second, first_new, second_new, code = refs[2 * places - 2 :]
    n_tok = part.shape[0]
    dot = functools.partial(
        lax.dot_general,
        dimension_numbers=(((0,), (0,)), ((), ())),
        preferred_element_type=jnp.float32,
    )
    projs = [part[...] + part_other[...]]
    for ref in coded:
        values = ref[:n_tok].astype(jnp.float32)
        scale = ref[n_tok : n_tok + 1, :].astype(jnp.float32)
        projs.append(decode(values, 1.0 / scale, code_squarings))
    p_high, p_low = split(jnp.concatenate(projs, axis=0))
    for k in range(2):
        parts = [own_grads[k]]
        for m in messages:
            values = m[k * n_tok : (k + 1) * n_tok].astype(jnp.float32)
            scale = values[:, share : share + 1]
            parts.append(decode(values, 1.0 / scale, code_squarings)[:, :share])
        g_high, g_low = split(jnp.concatenate(parts, axis=0))
        gradient = dot(g_high, p_high) + (dot(g_high, p_low) + dot(g_low, p_high))
        m = beta_first * first[k] + (1.0 - beta_first) * gradient
        v = beta_second * second[k] + (1.0 - beta_second) * gradient * gradient
        first_new[k] = m
        second_new[k] = v
        code[k] = encode(m / (jnp.sqrt(v) + adam_epsilon), code_scale, code_scale_squarings)


def moments_in_kernel(first, second, first_out, second_out):
    for k in range(2):
        first_out[k] = first[:, k]
        second_out[k] = second[:, k]


def moments_kernel(first, second, first_out, second_out):
    for k in range(2):
        first_out[:, k] = first[k]
        second_out[:, k] = second[k]


def lift_kernel(share, pieces, *refs):
    codes = refs[: len(pieces)]
    basis, master = refs[len(pieces) : len(pieces) + 2]
    out, o_buf, sem = refs[-3:]
    core = lax.rem(lax.axis_index("dp"), 2)
    plane = lax.div(lax.axis_index("dp"), 2)
    copies = []
    for k in range(2):
        values = jnp.concatenate([c[k] for c in codes], axis=0).astype(jnp.float32)
        terms = split(decode(values, step_size / code_scale, code_scale_squarings))
        lifted = jnp.dot(
            jnp.concatenate(terms, axis=1), basis[...], preferred_element_type=jnp.float32
        )
        for i, (j, other) in enumerate(pieces):
            who = 2 * jnp.bitwise_xor(plane, j) + jnp.bitwise_xor(core, other)
            row = pl.ds(pl.multiple_of(who * share, 16), share)
            o_buf[k, i] = master[k, row, :] - lifted[i * share : (i + 1) * share]
            c = pltpu.make_async_copy(o_buf.at[k, i], out.at[k, row], sem.at[k, i])
            c.start()
            copies.append(c)
    for c in copies:
        c.wait()


def fast_device(n_dp, n_hid, tokens, cotangent, weights, basis, master, first_moment, second_moment):
    places = n_dp // 2
    rows, width = tokens.shape
    group = rows * n_hid
    ff = weights.shape[1]
    share = ff // n_dp
    depth, rank = basis.shape
    f32, bf16 = jnp.float32, jnp.bfloat16

    def swap(x, axis, flip):
        n = n_hid if axis == "hid" else n_dp
        return lax.ppermute(x, axis, [(i, i ^ flip) for i in range(n)])

    def swap_hid(x, k):
        return swap(x, "hid", k)

    def swap_plane(x, j):
        return swap(x, "dp", 2 * j) if j else x

    def swap_core(x):
        return swap(x, "dp", 1)

    own = [tokens] + [swap_hid(tokens, k) for k in range(n_hid - 1, 0, -1)][::-1]
    bases = [basis] + [swap_plane(basis, j) for j in range(1, places)]

    cot_shape = jax.ShapeDtypeStruct((places, group, share), bf16)
    cot_own, cot_send = pl.pallas_call(
        functools.partial(cotangents_kernel, share, places),
        in_specs=[VMEM],
        out_specs=[VMEM] * 2,
        out_shape=[cot_shape] * 2,
        compiler_params=pltpu.CompilerParams(vmem_limit_bytes=4 * MIB),
        cost_estimate=SMALL,
        name="cotangents",
    )(cotangent)
    cot_other = swap_core(cot_send)

    held = pl.pallas_call(
        functools.partial(load_weights_kernel, share, places),
        in_specs=[HBM],
        out_specs=VMEM,
        out_shape=pltpu.VMEM((places, 2, share, width), bf16),
        scratch_shapes=[pltpu.SemaphoreType.DMA((places,))],
        compiler_params=pltpu.CompilerParams(vmem_limit_bytes=MIB),
        cost_estimate=pl.CostEstimate(
            flops=0, bytes_accessed=2 * places * 2 * share * width * 2, transcendentals=0
        ),
        name="load_weights",
    )(pltpu.with_memory_space_constraint(weights, pltpu.HBM))

    other = [swap_core(t) for t in own]
    messages = {}
    n_tok, spare = 2 * group, 16
    for j in list(range(places - 1, -1, -1)):
        first = j == places - 1
        ins = (own + other if first else [toks]) + [held, cot_own, cot_other]
        if j:
            shapes = [jax.ShapeDtypeStruct((2 * n_tok, rank), bf16)]
        else:
            shapes = [jax.ShapeDtypeStruct((2, n_tok, share), f32)]
        if first:
            shapes.append(jax.ShapeDtypeStruct((n_tok, width), bf16))
        outs = pl.pallas_call(
            functools.partial(grads_kernel, j, n_hid, rows, first),
            in_specs=[VMEM] * len(ins),
            out_specs=[VMEM] * len(shapes),
            out_shape=shapes,
            compiler_params=pltpu.CompilerParams(vmem_limit_bytes=6 * MIB),
            cost_estimate=pl.CostEstimate(
                flops=2 * n_tok * 2 * share * width,
                bytes_accessed=2 * share * width * 2,
                transcendentals=n_tok * share,
            )
            if j
            else SMALL,
        )(*ins)
        messages[j] = swap_plane(outs[0], j)
        if first:
            toks = outs[1]

    part_shape = jax.ShapeDtypeStruct((n_tok, rank), f32)
    part, part_send = pl.pallas_call(
        functools.partial(project_kernel, places),
        in_specs=[VMEM] * (1 + places),
        out_specs=[VMEM] * 2,
        out_shape=[part_shape] * 2,
        compiler_params=pltpu.CompilerParams(vmem_limit_bytes=6 * MIB),
        cost_estimate=pl.CostEstimate(
            flops=2 * n_tok * places * depth * rank,
            bytes_accessed=n_tok * width * 2,
            transcendentals=0,
        ),
        name="project",
    )(toks, *bases)
    part_other = swap_core(part_send)
    coded, basis_twice = pl.pallas_call(
        code_projected_kernel,
        in_specs=[VMEM] * 3,
        out_specs=[VMEM] * 2,
        out_shape=[
            jax.ShapeDtypeStruct((n_tok + spare, rank), bf16),
            jax.ShapeDtypeStruct((2 * rank, depth), bf16),
        ],
        compiler_params=pltpu.CompilerParams(vmem_limit_bytes=8 * MIB),
        cost_estimate=SMALL,
        name="code_projected",
    )(part, part_other, basis)

    half = jax.ShapeDtypeStruct((2, share, rank), f32)
    first_held, second_held = pl.pallas_call(
        moments_in_kernel,
        in_specs=[VMEM] * 2,
        out_specs=[VMEM] * 2,
        out_shape=[half] * 2,
        compiler_params=pltpu.CompilerParams(vmem_limit_bytes=8 * MIB),
        cost_estimate=SMALL,
        name="moments_in",
    )(first_moment, second_moment)
    first_new, second_new, code = pl.pallas_call(
        functools.partial(adam_kernel, places, share),
        in_specs=[VMEM] * (2 * places + 3),
        out_specs=[VMEM] * 3,
        out_shape=[half, half, jax.ShapeDtypeStruct((2, share, rank), bf16)],
        compiler_params=pltpu.CompilerParams(vmem_limit_bytes=12 * MIB),
        cost_estimate=SMALL,
        name="adam",
    )(
        messages[0],
        part,
        part_other,
        *[messages[j] for j in range(1, places)],
        *[swap_plane(coded, j) for j in range(1, places)],
        first_held,
        second_held,
    )

    codes = [swap_plane(code, j) for j in range(places)]
    moment_shape = jax.ShapeDtypeStruct((share, 2, rank), f32)
    first_new, second_new = pl.pallas_call(
        moments_kernel,
        in_specs=[VMEM] * 2,
        out_specs=[VMEM] * 2,
        out_shape=[moment_shape] * 2,
        compiler_params=pltpu.CompilerParams(vmem_limit_bytes=8 * MIB),
        cost_estimate=SMALL,
        name="moments",
    )(first_new, second_new)
    pieces = {(j, 0): codes[j] for j in range(places)}
    pieces.update({(j, 1): swap_core(codes[j]) for j in range(places)})
    master_new = None
    for some in lift_groups(places):
        kept = () if master_new is None else (master_new,)
        ins = [pieces[at] for at in some] + [basis_twice, master]
        master_new = pl.pallas_call(
            functools.partial(lift_kernel, share, some),
            in_specs=[VMEM] * len(ins) + [HBM] * len(kept),
            out_specs=HBM,
            out_shape=jax.ShapeDtypeStruct(master.shape, f32),
            scratch_shapes=[
                pltpu.VMEM((2, len(some), share, depth), f32),
                pltpu.SemaphoreType.DMA((2, len(some))),
            ],
            input_output_aliases={len(ins): 0} if kept else {},
            compiler_params=pltpu.CompilerParams(vmem_limit_bytes=12 * MIB),
            cost_estimate=pl.CostEstimate(
                flops=2 * 2 * 2 * len(some) * share * rank * depth,
                bytes_accessed=2 * 2 * len(some) * share * depth * 4,
                transcendentals=4 * len(some) * share * rank,
            ),
        )(*ins, *kept)
    return master_new, first_new, second_new


def plain_device(tokens, cotangent, weights, basis, master, first_moment, second_moment):
    highest = lax.Precision.HIGHEST
    group_tokens = lax.all_gather(tokens, "hid", axis=0, tiled=True)
    projected = jnp.dot(
        group_tokens,
        lax.all_gather(basis, "dp", axis=0, tiled=True),
        preferred_element_type=jnp.float32,
    )
    contract_cols = (((1,), (1,)), ((), ()))
    pre_gate = lax.dot_general(
        group_tokens, weights[0], contract_cols, preferred_element_type=jnp.float32
    )
    pre_up = lax.dot_general(
        group_tokens, weights[1], contract_cols, preferred_element_type=jnp.float32
    )
    activated, silu_slope = silu_pieces(pre_gate)
    upstream = cotangent.astype(jnp.float32)
    grad_gate = upstream * pre_up * silu_slope
    grad_up = upstream * activated
    over_tokens = (((0,), (0,)), ((), ()))
    gate_term = lax.dot_general(
        grad_gate, projected, over_tokens, precision=highest, preferred_element_type=jnp.float32
    )
    up_term = lax.dot_general(
        grad_up, projected, over_tokens, precision=highest, preferred_element_type=jnp.float32
    )
    gradient = lax.psum_scatter(
        jnp.stack([gate_term, up_term], axis=1), "dp", scatter_dimension=0, tiled=True
    )
    first_new = beta_first * first_moment + (1.0 - beta_first) * gradient
    second_new = beta_second * second_moment + (1.0 - beta_second) * gradient * gradient
    direction_share = first_new / (jnp.sqrt(second_new) + adam_epsilon)
    direction = lax.all_gather(direction_share, "dp", axis=0, tiled=True)
    lifted = jnp.einsum("fwr,dr->wfd", direction, basis.astype(jnp.float32), precision=highest)
    master_new = master - step_size * lifted
    return (master_new, first_new, second_new)


def lift_groups(places):
    groups = [[(j, 0), (j, 1)] for j in range(places - 2)]
    return groups + [[(j, other) for j in (places - 2, places - 1)] for other in range(2)]


def power_of_two(n):
    return n & (n - 1) == 0


def solution(mesh):
    n_dp, n_hid = mesh.shape["dp"], mesh.shape["hid"]

    def on_device(tokens, cotangent, weights, *rest):
        share = weights.shape[1] // n_dp
        aligned = share % 16 == 0 and tokens.shape[0] % 16 == 0 and rest[0].shape[0] % 128 == 0
        aligned = aligned and rest[0].shape[1] == (share // 128 + 1) * 128
        few = n_dp == 8 and power_of_two(n_hid) and n_hid <= 8
        if aligned and few:
            return fast_device(n_dp, n_hid, tokens, cotangent, weights, *rest)
        return plain_device(tokens, cotangent, weights, *rest)

    in_specs = (
        P(("dp", "hid"), None),
        P("dp", "hid"),
        P(None, "hid", None),
        P("dp", None),
        P(None, "hid", "dp"),
        P(("hid", "dp"), None, None),
        P(("hid", "dp"), None, None),
    )
    out_specs = (P(None, "hid", "dp"), P(("hid", "dp"), None, None), P(("hid", "dp"), None, None))
    return jax.shard_map(
        on_device, mesh=mesh, in_specs=in_specs, out_specs=out_specs, check_vma=False
    )
```

```python
import functools

import jax
import jax.numpy as jnp
from jax import lax
from jax.experimental import pallas as pl
from jax.experimental.pallas import tpu as pltpu
from jax.sharding import PartitionSpec as P


beta_first = 0.9
beta_second = 0.95
step_size = 0.05
adam_epsilon = 1e-08
code_scale = 4096.0
code_scale_squarings = 3
code_top = 240.0
code_squarings = 4
tiny = 1e-30


VMEM = pl.BlockSpec(memory_space=pltpu.VMEM)
HBM = pl.BlockSpec(memory_space=pltpu.HBM)
SMALL = pl.CostEstimate(flops=1000, bytes_accessed=1000, transcendentals=0)
MIB = 1 << 20


def silu_pieces(pre_gate):
    sigmoid_val = jax.nn.sigmoid(pre_gate)
    return (pre_gate * sigmoid_val, sigmoid_val * (1.0 + pre_gate * (1.0 - sigmoid_val)))


def split(x):
    high = x.astype(jnp.bfloat16)
    return high, (x - high.astype(jnp.float32)).astype(jnp.bfloat16)


def encode(x, scale, squarings):
    a = jnp.abs(x) * scale
    for _ in range(squarings):
        a = a * a
    return jnp.where(x < 0, -a, a).astype(jnp.bfloat16)


def decode(y, inverse_scale, squarings):
    a = jnp.abs(y)
    root = jnp.exp(jnp.log(a) * 0.5**squarings) * inverse_scale
    return jnp.where(y < 0, -root, root)


def scale_for(*terms):
    most = functools.reduce(jnp.maximum, [jnp.max(jnp.abs(t)) for t in terms])
    return (code_top / jnp.maximum(jnp.full((1, 1), most), tiny)).astype(jnp.bfloat16)


def load_weights_kernel(share, places, w_hbm, out, sem):
    core = lax.rem(lax.axis_index("dp"), 2)
    plane = lax.div(lax.axis_index("dp"), 2)
    copies = []
    for j in range(places):
        row = pl.multiple_of((2 * jnp.bitwise_xor(plane, j) + core) * share, 16)
        copies.append(
            pltpu.make_async_copy(w_hbm.at[:, pl.ds(row, share)], out.at[j], sem.at[j])
        )
    for c in copies:
        c.start()
    for c in copies:
        c.wait()


def cotangents_kernel(share, places, cot, own, send):
    core = lax.rem(lax.axis_index("dp"), 2)
    for c in range(2):

        @pl.when(core == c)
        def _():
            for p in range(places):
                here, there = 2 * p + c, 2 * p + 1 - c
                own[p] = cot[:, here * share : (here + 1) * share]
                send[p] = cot[:, there * share : (there + 1) * share]


def project_kernel(places, tok, *refs):
    bases = refs[:places]
    out_part, out_send = refs[places:]
    core = lax.rem(lax.axis_index("dp"), 2)
    plane = lax.div(lax.axis_index("dp"), 2)
    depth = bases[0].shape[0]
    total = None
    for j in range(places):
        col = pl.multiple_of((2 * jnp.bitwise_xor(plane, j) + core) * depth, 128)
        term = jnp.dot(tok[:, pl.ds(col, depth)], bases[j][...], preferred_element_type=jnp.float32)
        total = term if total is None else total + term
    half = total.shape[0] // 2
    out_part[...] = total
    out_send[:half] = total[half:]
    out_send[half:] = total[:half]


def grads_kernel(j, n_hid, rows, with_tokens, *refs):
    pieces = 2 * n_hid if with_tokens else 1
    toks, (w, cot_own, cot_other) = refs[:pieces], refs[pieces : pieces + 3]
    out = refs[pieces + 3]
    tok = toks[0]
    if with_tokens:
        tok = refs[-1]
        for i, t in enumerate(toks):
            tok[i * rows : (i + 1) * rows] = t[...]
    contract = (((1,), (1,)), ((), ()))
    plane = lax.div(lax.axis_index("dp"), 2)
    hid = lax.axis_index("hid")
    gate = lax.dot_general(tok[...], w[j, 0], contract, preferred_element_type=jnp.float32)
    up = lax.dot_general(tok[...], w[j, 1], contract, preferred_element_type=jnp.float32)
    place = jnp.bitwise_xor(plane, j)
    parts = []
    for cot in (cot_own, cot_other):
        for k in range(n_hid):
            start = pl.multiple_of(jnp.bitwise_xor(hid, k) * rows, rows)
            parts.append(cot[place, pl.ds(start, rows), :])
    upstream = jnp.concatenate(parts, axis=0).astype(jnp.float32)
    activated, slope = silu_pieces(gate)
    terms = (upstream * up * slope, upstream * activated)
    n_tok, share = gate.shape
    if j == 0:
        out[0], out[1] = terms
        return
    scale = scale_for(*terms)
    wide = scale.astype(jnp.float32)
    for k in range(2):
        here = slice(k * n_tok, (k + 1) * n_tok)
        out[here, :share] = encode(terms[k], wide, code_squarings)
        out[here, share:] = jnp.broadcast_to(scale, (n_tok, out.shape[1] - share))


def code_projected_kernel(part, part_other, basis, out, basis_twice):
    n_tok = part.shape[0]
    projected = part[...] + part_other[...]
    scale = scale_for(projected)
    out[:n_tok] = encode(projected, scale.astype(jnp.float32), code_squarings)
    out[n_tok:] = jnp.broadcast_to(scale, (out.shape[0] - n_tok, out.shape[1]))
    turned = basis[...].T
    rank = turned.shape[0]
    basis_twice[:rank] = turned
    basis_twice[rank:] = turned


def unpack_message(message, k, n_tok, share):
    values = message[k * n_tok : (k + 1) * n_tok].astype(jnp.float32)
    scale = values[:, share : share + 1]
    return split(decode(values, 1.0 / scale, code_squarings)[:, :share])


def unpack_kernel(places, own_grads, part, part_other, *refs):
    messages, coded = refs[: places - 2], refs[places - 2 : 2 * places - 3]
    g_high, g_low, p_high, p_low = refs[-4:]
    _, n_tok, share = own_grads.shape
    for j in range(places):
        here = slice(j * n_tok, (j + 1) * n_tok)
        if j:
            ref = coded[j - 1]
            scale = ref[n_tok : n_tok + 1, :].astype(jnp.float32)
            values = decode(ref[:n_tok].astype(jnp.float32), 1.0 / scale, code_squarings)
        else:
            values = part[...] + part_other[...]
        p_high[here], p_low[here] = split(values)
        for k in range(2):
            if j == 0:
                g_high[k, here], g_low[k, here] = split(own_grads[k])
            elif j < places - 1:
                g_high[k, here], g_low[k, here] = unpack_message(messages[j - 1], k, n_tok, share)


def adam_kernel(message, g_high, g_low, p_high, p_low, first, second, first_new, second_new, code):
    n_tok, share = message.shape[0] // 2, g_high.shape[2]
    dot = functools.partial(
        lax.dot_general,
        dimension_numbers=(((0,), (0,)), ((), ())),
        preferred_element_type=jnp.float32,
    )
    for k in range(2):
        last_high, last_low = unpack_message(message, k, n_tok, share)
        high = jnp.concatenate([g_high[k], last_high], axis=0)
        low = jnp.concatenate([g_low[k], last_low], axis=0)
        gradient = dot(high, p_high[...]) + (dot(high, p_low[...]) + dot(low, p_high[...]))
        m = beta_first * first[k] + (1.0 - beta_first) * gradient
        v = beta_second * second[k] + (1.0 - beta_second) * gradient * gradient
        first_new[k] = m
        second_new[k] = v
        code[k] = encode(m / (jnp.sqrt(v) + adam_epsilon), code_scale, code_scale_squarings)


def moments_in_kernel(first, second, first_out, second_out):
    for k in range(2):
        first_out[k] = first[:, k]
        second_out[k] = second[:, k]


def moments_kernel(first, second, first_out, second_out):
    for k in range(2):
        first_out[:, k] = first[k]
        second_out[:, k] = second[k]


def pick_kernel(from_first, from_second, out):
    core = lax.rem(lax.axis_index("dp"), 2)
    for c, ref in enumerate((from_first, from_second)):

        @pl.when(core == c)
        def _():
            out[...] = ref[...]


def lift_kernel(share, pieces, *refs):
    codes = refs[: len(pieces)]
    basis, master = refs[len(pieces) : len(pieces) + 2]
    out, o_buf, sem = refs[-3:]
    core = lax.rem(lax.axis_index("dp"), 2)
    plane = lax.div(lax.axis_index("dp"), 2)
    copies = []
    for first in range(len(pieces)):
        some = list(enumerate(pieces))[first : first + 1]
        for k in range(2):
            values = jnp.concatenate([codes[i][k] for i, _ in some], axis=0).astype(jnp.float32)
            terms = split(decode(values, step_size / code_scale, code_scale_squarings))
            lifted = jnp.dot(
                jnp.concatenate(terms, axis=1), basis[...], preferred_element_type=jnp.float32
            )
            for i, (j, other) in some:
                who = 2 * jnp.bitwise_xor(plane, j) + jnp.bitwise_xor(core, other)
                row = pl.ds(pl.multiple_of(who * share, 16), share)
                at = i - first
                o_buf[k, i] = master[k, row, :] - lifted[at * share : (at + 1) * share]
                c = pltpu.make_async_copy(o_buf.at[k, i], out.at[k, row], sem.at[k, i])
                c.start()
                copies.append(c)
    for c in copies:
        c.wait()


def fast_device(n_dp, n_hid, tokens, cotangent, weights, basis, master, first_moment, second_moment):
    places = n_dp // 2
    rows, width = tokens.shape
    group = rows * n_hid
    ff = weights.shape[1]
    share = ff // n_dp
    depth, rank = basis.shape
    f32, bf16 = jnp.float32, jnp.bfloat16

    def swap(x, axis, flip):
        n = n_hid if axis == "hid" else n_dp
        return lax.ppermute(x, axis, [(i, i ^ flip) for i in range(n)])

    def swap_hid(x, k):
        return swap(x, "hid", k)

    def swap_plane(x, j):
        return swap(x, "dp", 2 * j) if j else x

    def swap_core(x):
        return swap(x, "dp", 1)

    own = [tokens] + [swap_hid(tokens, k) for k in range(n_hid - 1, 0, -1)][::-1]
    bases = [basis] + [swap_plane(basis, j) for j in range(1, places)]

    cot_shape = jax.ShapeDtypeStruct((places, group, share), bf16)
    cot_own, cot_send = pl.pallas_call(
        functools.partial(cotangents_kernel, share, places),
        in_specs=[VMEM],
        out_specs=[VMEM] * 2,
        out_shape=[cot_shape] * 2,
        compiler_params=pltpu.CompilerParams(vmem_limit_bytes=4 * MIB),
        cost_estimate=SMALL,
        name="cotangents",
    )(cotangent)
    cot_other = swap_core(cot_send)

    held = pl.pallas_call(
        functools.partial(load_weights_kernel, share, places),
        in_specs=[HBM],
        out_specs=VMEM,
        out_shape=pltpu.VMEM((places, 2, share, width), bf16),
        scratch_shapes=[pltpu.SemaphoreType.DMA((places,))],
        compiler_params=pltpu.CompilerParams(vmem_limit_bytes=MIB),
        cost_estimate=pl.CostEstimate(
            flops=0, bytes_accessed=2 * places * 2 * share * width * 2, transcendentals=0
        ),
        name="load_weights",
    )(pltpu.with_memory_space_constraint(weights, pltpu.HBM))

    other = [swap_core(t) for t in own]
    messages = {}
    n_tok, spare = 2 * group, 16
    for j in range(places - 1, -1, -1):
        first = j == places - 1
        ins = (own + other if first else [toks]) + [held, cot_own, cot_other]
        if j:
            shapes = [jax.ShapeDtypeStruct((2 * n_tok, rank), bf16)]
        else:
            shapes = [jax.ShapeDtypeStruct((2, n_tok, share), f32)]
        if first:
            shapes.append(jax.ShapeDtypeStruct((n_tok, width), bf16))
        outs = pl.pallas_call(
            functools.partial(grads_kernel, j, n_hid, rows, first),
            in_specs=[VMEM] * len(ins),
            out_specs=[VMEM] * len(shapes),
            out_shape=shapes,
            compiler_params=pltpu.CompilerParams(vmem_limit_bytes=6 * MIB),
            cost_estimate=pl.CostEstimate(
                flops=2 * n_tok * 2 * share * width,
                bytes_accessed=2 * share * width * 2,
                transcendentals=n_tok * share,
            )
            if j
            else SMALL,
        )(*ins)
        messages[j] = swap_plane(outs[0], j)
        if first:
            toks = outs[1]

    part_shape = jax.ShapeDtypeStruct((n_tok, rank), f32)
    part, part_send = pl.pallas_call(
        functools.partial(project_kernel, places),
        in_specs=[VMEM] * (1 + places),
        out_specs=[VMEM] * 2,
        out_shape=[part_shape] * 2,
        compiler_params=pltpu.CompilerParams(vmem_limit_bytes=6 * MIB),
        cost_estimate=pl.CostEstimate(
            flops=2 * n_tok * places * depth * rank,
            bytes_accessed=n_tok * width * 2,
            transcendentals=0,
        ),
        name="project",
    )(toks, *bases)
    part_other = swap_core(part_send)
    coded, basis_twice = pl.pallas_call(
        code_projected_kernel,
        in_specs=[VMEM] * 3,
        out_specs=[VMEM] * 2,
        out_shape=[
            jax.ShapeDtypeStruct((n_tok + spare, rank), bf16),
            jax.ShapeDtypeStruct((2 * rank, depth), bf16),
        ],
        compiler_params=pltpu.CompilerParams(vmem_limit_bytes=8 * MIB),
        cost_estimate=SMALL,
        name="code_projected",
    )(part, part_other, basis)

    half = jax.ShapeDtypeStruct((2, share, rank), f32)
    first_held, second_held = pl.pallas_call(
        moments_in_kernel,
        in_specs=[VMEM] * 2,
        out_specs=[VMEM] * 2,
        out_shape=[half] * 2,
        compiler_params=pltpu.CompilerParams(vmem_limit_bytes=8 * MIB),
        cost_estimate=SMALL,
        name="moments_in",
    )(first_moment, second_moment)
    senders = list(range(places - 1, 1, -1))
    g_shape = jax.ShapeDtypeStruct((2, (places - 1) * n_tok, share), bf16)
    p_shape = jax.ShapeDtypeStruct((places * n_tok, rank), bf16)
    terms = pl.pallas_call(
        functools.partial(unpack_kernel, places),
        in_specs=[VMEM] * (2 * places),
        out_specs=[VMEM] * 4,
        out_shape=[g_shape, g_shape, p_shape, p_shape],
        compiler_params=pltpu.CompilerParams(vmem_limit_bytes=8 * MIB),
        cost_estimate=SMALL,
        name="unpack",
    )(
        messages[0],
        part,
        part_other,
        *[messages[j] for j in senders],
        *[swap_plane(coded, j) for j in senders + [1]],
    )
    first_new, second_new, code = pl.pallas_call(
        adam_kernel,
        in_specs=[VMEM] * 7,
        out_specs=[VMEM] * 3,
        out_shape=[half, half, jax.ShapeDtypeStruct((2, share, rank), bf16)],
        compiler_params=pltpu.CompilerParams(vmem_limit_bytes=12 * MIB),
        cost_estimate=SMALL,
        name="adam",
    )(messages[1], *terms, first_held, second_held)

    codes = [swap_plane(code, j) for j in range(places - 1)]
    relay = pl.pallas_call(
        pick_kernel,
        in_specs=[VMEM] * 2,
        out_specs=VMEM,
        out_shape=jax.ShapeDtypeStruct((2, share, rank), bf16),
        compiler_params=pltpu.CompilerParams(vmem_limit_bytes=2 * MIB),
        cost_estimate=SMALL,
        name="pick",
    )(codes[1], codes[2])
    flips = [4 if i % 2 == 0 else 2 for i in range(n_dp)]
    codes.append(lax.ppermute(relay, "dp", [(i, i ^ flips[i]) for i in range(n_dp)]))
    moment_shape = jax.ShapeDtypeStruct((share, 2, rank), f32)
    first_new, second_new = pl.pallas_call(
        moments_kernel,
        in_specs=[VMEM] * 2,
        out_specs=[VMEM] * 2,
        out_shape=[moment_shape] * 2,
        compiler_params=pltpu.CompilerParams(vmem_limit_bytes=8 * MIB),
        cost_estimate=SMALL,
        name="moments",
    )(first_new, second_new)
    pieces = {(j, 0): codes[j] for j in range(places)}
    pieces.update({(j, 1): swap_core(codes[j]) for j in range(places)})
    master_new = None
    for some in lift_groups(places):
        kept = () if master_new is None else (master_new,)
        ins = [pieces[at] for at in some] + [basis_twice, master]
        master_new = pl.pallas_call(
            functools.partial(lift_kernel, share, some),
            in_specs=[VMEM] * len(ins) + [HBM] * len(kept),
            out_specs=HBM,
            out_shape=jax.ShapeDtypeStruct(master.shape, f32),
            scratch_shapes=[
                pltpu.VMEM((2, len(some), share, depth), f32),
                pltpu.SemaphoreType.DMA((2, len(some))),
            ],
            input_output_aliases={len(ins): 0} if kept else {},
            compiler_params=pltpu.CompilerParams(vmem_limit_bytes=12 * MIB),
            cost_estimate=pl.CostEstimate(
                flops=2 * 2 * 2 * len(some) * share * rank * depth,
                bytes_accessed=2 * 2 * len(some) * share * depth * 4,
                transcendentals=4 * len(some) * share * rank,
            ),
        )(*ins, *kept)
    return master_new, first_new, second_new


def plain_device(tokens, cotangent, weights, basis, master, first_moment, second_moment):
    highest = lax.Precision.HIGHEST
    group_tokens = lax.all_gather(tokens, "hid", axis=0, tiled=True)
    projected = jnp.dot(
        group_tokens,
        lax.all_gather(basis, "dp", axis=0, tiled=True),
        preferred_element_type=jnp.float32,
    )
    contract_cols = (((1,), (1,)), ((), ()))
    pre_gate = lax.dot_general(
        group_tokens, weights[0], contract_cols, preferred_element_type=jnp.float32
    )
    pre_up = lax.dot_general(
        group_tokens, weights[1], contract_cols, preferred_element_type=jnp.float32
    )
    activated, silu_slope = silu_pieces(pre_gate)
    upstream = cotangent.astype(jnp.float32)
    grad_gate = upstream * pre_up * silu_slope
    grad_up = upstream * activated
    over_tokens = (((0,), (0,)), ((), ()))
    gate_term = lax.dot_general(
        grad_gate, projected, over_tokens, precision=highest, preferred_element_type=jnp.float32
    )
    up_term = lax.dot_general(
        grad_up, projected, over_tokens, precision=highest, preferred_element_type=jnp.float32
    )
    gradient = lax.psum_scatter(
        jnp.stack([gate_term, up_term], axis=1), "dp", scatter_dimension=0, tiled=True
    )
    first_new = beta_first * first_moment + (1.0 - beta_first) * gradient
    second_new = beta_second * second_moment + (1.0 - beta_second) * gradient * gradient
    direction_share = first_new / (jnp.sqrt(second_new) + adam_epsilon)
    direction = lax.all_gather(direction_share, "dp", axis=0, tiled=True)
    lifted = jnp.einsum("fwr,dr->wfd", direction, basis.astype(jnp.float32), precision=highest)
    master_new = master - step_size * lifted
    return (master_new, first_new, second_new)


def lift_groups(places):
    last = places - 1
    middle = [[(j, other) for j in range(1, last)] for other in range(2)]
    return [[(0, 0), (0, 1)]] + middle + [[(last, 0)], [(last, 1)]]


def power_of_two(n):
    return n & (n - 1) == 0


def solution(mesh):
    n_dp, n_hid = mesh.shape["dp"], mesh.shape["hid"]

    def on_device(tokens, cotangent, weights, *rest):
        share = weights.shape[1] // n_dp
        aligned = share % 16 == 0 and tokens.shape[0] % 16 == 0 and rest[0].shape[0] % 128 == 0
        aligned = aligned and rest[0].shape[1] == (share // 128 + 1) * 128
        few = n_dp == 8 and power_of_two(n_hid) and n_hid <= 8
        if aligned and few:
            return fast_device(n_dp, n_hid, tokens, cotangent, weights, *rest)
        return plain_device(tokens, cotangent, weights, *rest)

    in_specs = (
        P(("dp", "hid"), None),
        P("dp", "hid"),
        P(None, "hid", None),
        P("dp", None),
        P(None, "hid", "dp"),
        P(("hid", "dp"), None, None),
        P(("hid", "dp"), None, None),
    )
    out_specs = (P(None, "hid", "dp"), P(("hid", "dp"), None, None), P(("hid", "dp"), None, None))
    return jax.shard_map(
        on_device, mesh=mesh, in_specs=in_specs, out_specs=out_specs, check_vma=False
    )
```
